32 devices in a mesh: segment: 4 (over y, x), tile: 8 (over z, core).
Axes of the slice: x: 2, y: 2, z: 4, core: 2. Of those that a mesh axis runs over, the one named last changes fastest.
Arguments:
- raw_frames: bfloat16 [32, 1280, 1280], P(('segment', 'tile')), may hold values from -6 to 6
- dark_frame: bfloat16 [1280, 1280], replicated, may hold values from -2.5 to 2.5
- flat_field: bfloat16 [1280, 1280], replicated, may hold values from 0.25 to 1.75
- seeing: float32 [32, 64], P(None, 'tile'), may hold values from 0.1 to 10
- anchors: int32 [64, 2], replicated, may hold values from 0 to 1023, as said below
- taper: int32 [64], replicated, may hold values from 16 to 64
Outputs:
- power: float32 [64, 256, 256], P('tile', 'segment')
- cross: float32 [64, 4, 256, 256], P('tile', None, 'segment')
The draws below stay inside these ranges and needn't reach their ends.
Inputs may be any that keep to these rules, and one draw needn't show every extreme that they name: `anchors`: the subfield g = 8 i + j has anchor (128 i + a, 128 j + b) with a and b below 128.
All inputs are finite; a program needn't handle non-finite values.
Results may differ from the reference program's by a relative error of at most 0.013.
Values may be sent and summed in bfloat16 or wider, within the bound.
No kernel may reach another device: no remote copies, remote signals or barrier semaphores. Data moves between devices by JAX's collectives and lax.ppermute only.
A program may use at most 192 MiB of HBM per device.

```python
import math
import jax
import jax.numpy as jnp
from jax import lax

S = 256
GRID = 8
STRIDE = 128
IMG = 1280
SUBFIELDS = 64
FRAMES = 32


def draw_anchors(key, part):
    jitter = jax.random.randint(key, (GRID, GRID, 2), 0, STRIDE)
    jitter = jitter.at[0, 0].set(0).at[GRID - 1, GRID - 1].set(STRIDE - 1)
    rows = jnp.broadcast_to(jnp.arange(GRID, dtype=jnp.int32)[:, None], (GRID, GRID))
    cols = jnp.broadcast_to(jnp.arange(GRID, dtype=jnp.int32)[None, :], (GRID, GRID))
    base = jnp.stack([rows, cols], axis=-1) * STRIDE
    return (base + jitter).reshape(GRID * GRID, 2).astype(jnp.int32)


def with_ends(result, stream_key, low, top_value):
    longest = result.shape.index(max(result.shape))
    spots = []
    for shift in (0, 1):
        where = [jax.random.randint(jax.random.fold_in(stream_key, axis), (), 0, length) for axis, length in enumerate(result.shape)]
        where[longest] = (where[longest] + shift) % result.shape[longest]
        spots.append(tuple(where))
    return result.at[spots[0]].set(low).at[spots[1]].set(top_value)


def steps_of(key, dims, pieces, smallest, top_value):
    def one(dim, blocks):
        heights = jax.random.uniform(jax.random.fold_in(jax.random.fold_in(key, 6), dim), (blocks,), jnp.float32, smallest / len(pieces), top_value / len(pieces))
        return jnp.repeat(jnp.exp(heights), dims[dim] // blocks).reshape((-1,) + (1,) * (len(dims) - dim - 1))

    loudness = one(*pieces[0])
    for cut in pieces[1:]:
        loudness = loudness * one(*cut)
    return loudness


def gaussian(rng, extent, spread, bound, shards=(), held_as=jnp.bfloat16):
    entries = jax.random.normal(rng, extent, jnp.float32) * spread
    if len(shards) > 0:
        entries = steps_of(rng, extent, shards, -0.22, 0.18) * entries
    return jnp.clip(entries, min=-bound, max=bound).astype(held_as)


def setup_inputs(seed: int = 0) -> dict:
    seeds = jax.random.split(jax.random.key(seed), 7)
    return {
        "raw_frames": gaussian(seeds[0], (FRAMES, IMG, IMG), 1.0, 6.0, ((0, 32),)),
        "dark_frame": gaussian(seeds[1], (IMG, IMG), 0.3, 2.5),
        "flat_field": jnp.clip(1.0 + 0.15 * jax.random.normal(seeds[2], (IMG, IMG), jnp.float32), 0.25, 1.75).astype(jnp.bfloat16),
        "seeing": jnp.clip(jnp.exp(math.log(10.0) - 4.6051702 * jax.random.uniform(seeds[3], (FRAMES, SUBFIELDS), jnp.float32) ** steps_of(seeds[3], (FRAMES, SUBFIELDS), ((1, 8),), -0.2, 0.2)), 0.1, 10.0),
        "anchors": draw_anchors(jax.random.fold_in(seeds[6], 71), 0),
        "taper": with_ends(jax.random.randint(seeds[5], (SUBFIELDS,), S // 16, S // 4 + 1), jax.random.fold_in(seeds[5], 1), S // 16, (S // 4 + 1) - 1).astype(jnp.int32),
    }


def ramp_rows(taper):
    place = jnp.arange(S, dtype=jnp.float32)
    width = taper.astype(jnp.float32)
    left = jnp.where(place < width, 0.5 - 0.5 * jnp.cos(jnp.pi * (place + 0.5) / width), 1.0)
    return left * left[::-1]

def reference(raw_frames, dark_frame, flat_field, seeing, anchors, taper):
    scale = jnp.sqrt(jnp.float32(S))

    def one_field(index):
        anchor = anchors[index]
        start = jnp.zeros((), jnp.int32)
        piece = lax.dynamic_slice(raw_frames, (start, anchor[0], anchor[1]), (FRAMES, S, S)).astype(jnp.float32)
        dark_piece = lax.dynamic_slice(dark_frame, (anchor[0], anchor[1]), (S, S)).astype(jnp.float32)
        flat_piece = lax.dynamic_slice(flat_field, (anchor[0], anchor[1]), (S, S)).astype(jnp.float32)
        cal = (piece - dark_piece[None]) / flat_piece[None]
        centered = cal - lax.optimization_barrier(jnp.mean(cal, axis=(1, 2), keepdims=True))
        ramp = ramp_rows(taper[index])
        sub = (centered * (ramp[:, None] * ramp[None, :])[None]).astype(jnp.bfloat16)
        first = jnp.fft.fft(sub.astype(jnp.float32), axis=2) / scale
        real_half = lax.optimization_barrier(jnp.real(first).astype(jnp.bfloat16)).astype(jnp.float32)
        imag_half = lax.optimization_barrier(jnp.imag(first).astype(jnp.bfloat16)).astype(jnp.float32)
        second = jnp.fft.fft(real_half + 1j * imag_half, axis=1) / scale
        real_part = jnp.real(second).astype(jnp.float32)
        imag_part = jnp.imag(second).astype(jnp.float32)
        weights = seeing[:, index]
        weight_sum = jnp.sum(weights)
        wgt = weights[:, None, None]
        power_sum = lax.optimization_barrier(jnp.sum(wgt * (real_part * real_part + imag_part * imag_part), axis=0))
        real_u = jnp.roll(real_part, -1, axis=1)
        imag_u = jnp.roll(imag_part, -1, axis=1)
        real_v = jnp.roll(real_part, -1, axis=2)
        imag_v = jnp.roll(imag_part, -1, axis=2)
        cross_sum = jnp.stack([lax.optimization_barrier(jnp.sum(wgt * (real_part * real_u + imag_part * imag_u), axis=0)), lax.optimization_barrier(jnp.sum(wgt * (imag_part * real_u - real_part * imag_u), axis=0)), lax.optimization_barrier(jnp.sum(wgt * (real_part * real_v + imag_part * imag_v), axis=0)), lax.optimization_barrier(jnp.sum(wgt * (imag_part * real_v - real_part * imag_v), axis=0))], axis=0)
        return (power_sum / weight_sum, cross_sum / weight_sum)
    power, cross = lax.map(one_field, jnp.arange(SUBFIELDS, dtype=jnp.int32))
    return (power, cross)
```

```python
import math

import jax
import jax.numpy as jnp
from jax import lax
from jax.experimental import pallas as pl
from jax.experimental.pallas import tpu as pltpu
from jax.sharding import PartitionSpec as P

S = 256
GROUP = 256
REGION = 384
HALF = 136
VMEM_LIMIT = 60000 * 1024


def ramp_rows(taper, size):
    place = jnp.arange(size, dtype=jnp.float32)[None, :]
    width = taper.astype(jnp.float32)[:, None]
    left = jnp.where(place < width, 0.5 - 0.5 * jnp.cos(jnp.pi * (place + 0.5) / width), 1.0)
    return left * left[:, ::-1]


def dft_tables(size):
    steps = jnp.arange(size, dtype=jnp.int32)
    phase = steps[:, None] * steps[None, :] % size
    angle = 2.0 * jnp.pi * phase.astype(jnp.float32) / size
    factor = 1.0 / jnp.sqrt(jnp.float32(size))
    return (
        (jnp.cos(angle) * factor).astype(jnp.bfloat16),
        (jnp.sin(angle) * factor).astype(jnp.bfloat16),
    )


def first_pass(sub, cosine, sine):
    table = jnp.concatenate([cosine, -sine], axis=1)
    return jnp.einsum("fsxy,yk->fsxk", sub, table, preferred_element_type=jnp.float32).astype(
        jnp.bfloat16
    )


def second_pass(half, cosine, sine):
    size = cosine.shape[0]
    with_cos = jnp.einsum("ux,fsxk->fsuk", cosine, half, preferred_element_type=jnp.float32)
    with_sin = jnp.einsum("ux,fsxk->fsuk", sine, half, preferred_element_type=jnp.float32)
    real_part = with_cos[..., :size] + with_sin[..., size:]
    imag_part = with_cos[..., size:] - with_sin[..., :size]
    return (real_part, imag_part)


def local_any(raw_frames, dark_frame, flat_field, seeing, anchors, taper):
    size = S
    cosine, sine = dft_tables(size)
    ramps = ramp_rows(taper, size)
    calibrated = (
        raw_frames.astype(jnp.float32) - dark_frame.astype(jnp.float32)[None]
    ) / flat_field.astype(jnp.float32)[None]

    def cutout(anchor, ramp):
        start = jnp.zeros((), jnp.int32)
        cal = lax.dynamic_slice(
            calibrated, (start, anchor[0], anchor[1]), (calibrated.shape[0], size, size)
        )
        centered = cal - jnp.mean(cal, axis=(1, 2), keepdims=True)
        return (centered * (ramp[:, None] * ramp[None, :])[None]).astype(jnp.bfloat16)

    sub = jax.vmap(cutout, in_axes=(0, 0), out_axes=1)(anchors, ramps)
    received = lax.all_to_all(sub, "tile", split_axis=1, concat_axis=0, tiled=True)
    n_frames = received.shape[0]
    sub_dev = received.shape[1]
    block = math.gcd(n_frames, 8)
    n_blocks = n_frames // block
    segment_index = lax.axis_index("segment")
    weights = lax.dynamic_slice_in_dim(seeing, segment_index * n_frames, n_frames, 0)
    weight_sum = jnp.sum(seeing, axis=0)
    blocks = received.reshape((n_blocks, block) + received.shape[1:])
    weight_blocks = weights.reshape(n_blocks, block, sub_dev)

    def accumulate(carry, inputs):
        data, wblock = inputs
        half = first_pass(data, cosine, sine)
        real_part, imag_part = second_pass(half, cosine, sine)
        wgt = wblock[:, :, None, None]
        power_sum = carry[0] + jnp.sum(
            wgt * (real_part * real_part + imag_part * imag_part), axis=0
        )
        real_u = jnp.roll(real_part, -1, axis=2)
        imag_u = jnp.roll(imag_part, -1, axis=2)
        real_v = jnp.roll(real_part, -1, axis=3)
        imag_v = jnp.roll(imag_part, -1, axis=3)
        cross_sum = carry[1] + jnp.stack(
            [
                jnp.sum(wgt * (real_part * real_u + imag_part * imag_u), axis=0),
                jnp.sum(wgt * (imag_part * real_u - real_part * imag_u), axis=0),
                jnp.sum(wgt * (real_part * real_v + imag_part * imag_v), axis=0),
                jnp.sum(wgt * (imag_part * real_v - real_part * imag_v), axis=0),
            ],
            axis=1,
        )
        return ((power_sum, cross_sum), None)

    start_power = jnp.zeros((sub_dev, size, size), jnp.float32)
    start_cross = jnp.zeros((sub_dev, 4, size, size), jnp.float32)
    (power_sum, cross_sum), unused = lax.scan(
        accumulate, (start_power, start_cross), (blocks, weight_blocks)
    )
    power_rows, cross_rows = (
        lax.psum_scatter(
            power_sum.astype(jnp.bfloat16), "segment", scatter_dimension=1, tiled=True
        ).astype(jnp.float32),
        lax.psum_scatter(
            cross_sum.astype(jnp.bfloat16), "segment", scatter_dimension=2, tiled=True
        ).astype(jnp.float32),
    )
    power = power_rows / weight_sum[:, None, None]
    cross = cross_rows / weight_sum[:, None, None, None]
    return (power, cross)


def shifted_ramps(taper, offset, length):
    place = jnp.arange(length, dtype=jnp.int32)[None, :] - offset[:, None]
    inside = (place >= 0) & (place < S)
    width = taper.astype(jnp.float32)[:, None]

    def side(spot):
        spot = spot.astype(jnp.float32)
        rise = 0.5 - 0.5 * jnp.cos(jnp.pi * (spot + 0.5) / width)
        return jnp.where(spot < width, rise, 1.0)

    return jnp.where(inside, side(place) * side(S - 1 - place), 0.0)


def spectra_kernel(
    scal, wgt, own0, own1, far0, far1, dark0, dark1, rate0, rate1, ramp, wave, table, out,
    cal, shifted, real, imag, sums,
):
    step = pl.program_id(0)
    pair = ramp.shape[0]
    segment = scal[0]

    @pl.when(step == 0)
    def _():
        sums[...] = jnp.zeros_like(sums)
        for j in range(pair):
            first = 128 - scal[4 + 2 * j + 1]
            for m in range(4):
                shifted[j, :, 128 * m : 128 * m + 128] = wave[m, pl.ds(first, REGION), :].astype(
                    jnp.bfloat16
                )

    lane = lax.broadcasted_iota(jnp.int32, (1, 128), 1)
    last_lane = lax.broadcasted_iota(jnp.int32, (8, 128), 1) == 127
    for near in range(2):
        for m in range(4):
            left = (own0, far0)[near] if m < 2 else (own1, far1)[near]
            dark = dark0 if m < 2 else dark1
            rate = rate0 if m < 2 else rate1
            cols = slice(128 * (m % 2), 128 * (m % 2) + 128)
            cal[near, m] = (left[0, :, cols].astype(jnp.float32) - dark[:, cols]) * rate[:, cols]
    for near in range(2):
        frame = scal[1] + 2 * step + (scal[2] if near == 0 else 1 - scal[2])
        for j in range(pair):
            top = scal[4 + 2 * j]
            left = scal[4 + 2 * j + 1]
            weight = wgt[frame, scal[3] + j]
            pieces = [cal[near, j + m, pl.ds(top, S), :] for m in range(3)]
            total = [jnp.sum(piece, axis=0, keepdims=True) for piece in pieces]
            total = (
                jnp.where(lane >= left, total[0], 0.0)
                + total[1]
                + jnp.where(lane < left, total[2], 0.0)
            )
            mean = jnp.sum(total, axis=1, keepdims=True) * (1.0 / (S * S))
            sub = jnp.concatenate(
                [
                    ((piece - mean) * ramp[j, :, 128 * m : 128 * m + 128]).astype(jnp.bfloat16)
                    for m, piece in enumerate(pieces)
                ],
                axis=1,
            )
            half = jnp.dot(sub, shifted[j], preferred_element_type=jnp.float32).astype(jnp.bfloat16)
            both = jnp.dot(table[...], half, preferred_element_type=jnp.float32)
            for m in range(2):
                lo = slice(128 * m, 128 * m + 128)
                hi = slice(S + 128 * m, S + 128 * m + 128)
                real[near, j, m] = both[:HALF, lo] + both[HALF:, hi]
                imag[near, j, m] = both[:HALF, hi] - both[HALF:, lo]
            for r in range(0, HALF, 8):
                rows = slice(r, r + 8)
                re = [real[near, j, m, rows, :] for m in range(2)]
                im = [imag[near, j, m, rows, :] for m in range(2)]
                re_s = [pltpu.roll(x, 127, 1) for x in re]
                im_s = [pltpu.roll(x, 127, 1) for x in im]
                for m in range(2):
                    wre = re[m] * weight
                    wim = im[m] * weight
                    sums[j, 0, m, rows, :] += wre * re[m] + wim * im[m]
                    if r < 128:
                        below = slice(r + 1, r + 9)
                        re_u = real[near, j, m, below, :]
                        im_u = imag[near, j, m, below, :]
                        sums[j, 1, m, rows, :] += wre * re_u + wim * im_u
                        sums[j, 2, m, rows, :] += wim * re_u - wre * im_u
                    re_v = jnp.where(last_lane, re_s[1 - m], re_s[m])
                    im_v = jnp.where(last_lane, im_s[1 - m], im_s[m])
                    sums[j, 3, m, rows, :] += wre * re_v + wim * im_v
                    sums[j, 4, m, rows, :] += wim * re_v - wre * im_v

    @pl.when(step == pl.num_programs(0) - 1)
    def _():
        for target in range(4):
            slot = jnp.bitwise_xor(segment, target)
            for j in range(pair):
                for plane in range(5):
                    first = (0, 64, 64, 0)[target]
                    if plane not in (1, 2):
                        first = (0, 64, 65, 1)[target]
                    for m in range(2):
                        out[slot, j, plane, :, 128 * m : 128 * m + 128] = sums[
                            j, plane, m, first : first + 64, :
                        ].astype(jnp.bfloat16)


def spectra(p, scal, seeing, own, far, dark, rate, ramp, wave, table):
    n = own[0].shape[0]
    frames = pl.BlockSpec((1, REGION, GROUP), lambda i, s: (i, 0, 0))
    left = pl.BlockSpec((REGION, GROUP), lambda i, s: (0, p))
    right = pl.BlockSpec((REGION, GROUP), lambda i, s: (0, p + 1))
    return pl.pallas_call(
        spectra_kernel,
        name="spectra",
        grid_spec=pltpu.PrefetchScalarGridSpec(
            num_scalar_prefetch=1,
            grid=(n,),
            in_specs=[
                pl.BlockSpec(memory_space=pltpu.SMEM),
                frames,
                frames,
                frames,
                frames,
                left,
                right,
                left,
                right,
                pl.BlockSpec((2, S, REGION), lambda i, s: (p, 0, 0)),
                pl.BlockSpec(wave.shape, lambda i, s: (0, 0, 0)),
                pl.BlockSpec(table.shape, lambda i, s: (0, 0)),
            ],
            out_specs=pl.BlockSpec((4, 2, 5, 64, S), lambda i, s: (0, 0, 0, 0, 0)),
            scratch_shapes=[
                pltpu.VMEM((2, 4, REGION, 128), jnp.float32),
                pltpu.VMEM((2, REGION, 2 * S), jnp.bfloat16),
                pltpu.VMEM((2, 2, 2, HALF, 128), jnp.float32),
                pltpu.VMEM((2, 2, 2, HALF, 128), jnp.float32),
                pltpu.VMEM((2, 5, 2, HALF, 128), jnp.float32),
            ],
        ),
        out_shape=jax.ShapeDtypeStruct((4, 2, 5, 64, S), jnp.bfloat16),
        compiler_params=pltpu.CompilerParams(
            dimension_semantics=("arbitrary",), vmem_limit_bytes=VMEM_LIMIT
        ),
    )(scal, seeing, own[0], own[1], far[0], far[1], dark, dark, rate, rate, ramp, wave, table)


def finish_kernel(mine, got1, got2, got3, flip, mix, inverse, *refs):
    power, cross = refs[-2:]
    for j in range(2):
        for plane in range(5):
            parts = jnp.concatenate([x[0, j, plane] for x in (mine, got1, got2, got3)], axis=0)
            turned = jnp.dot(
                parts, flip[1 if plane >= 3 else 0], preferred_element_type=jnp.float32
            ).astype(jnp.bfloat16)
            total = jnp.dot(mix[...], turned, preferred_element_type=jnp.float32)
            total = total * inverse[j]
            if plane == 0:
                power[j] = total
            else:
                cross[j, plane - 1] = total


def finish(p, parts, flip, mix, inverse, before, n_sub):
    part = pl.BlockSpec((1, 2, 5, 64, S), lambda i: (0, 0, 0, 0, 0))
    specs = [part] * 4 + [
        pl.BlockSpec((2, S, S), lambda i: (0, 0, 0)),
        pl.BlockSpec((64, S), lambda i: (0, 0)),
        pl.BlockSpec((2, 1, S), lambda i: (p, 0, 0)),
    ]
    aliases = {}
    if before is not None:
        specs += [pl.BlockSpec(memory_space=pl.ANY)] * 2
        aliases = {7: 0, 8: 1}
    return pl.pallas_call(
        finish_kernel,
        name="finish",
        grid=(1,),
        in_specs=specs,
        out_specs=[
            pl.BlockSpec((2, 64, S), lambda i: (p, 0, 0)),
            pl.BlockSpec((2, 4, 64, S), lambda i: (p, 0, 0, 0)),
        ],
        out_shape=[
            jax.ShapeDtypeStruct((n_sub, 64, S), jnp.float32),
            jax.ShapeDtypeStruct((n_sub, 4, 64, S), jnp.float32),
        ],
        input_output_aliases=aliases,
        compiler_params=pltpu.CompilerParams(vmem_limit_bytes=VMEM_LIMIT),
    )(*parts, flip, mix, inverse, *(before or ()))


def local_rows(raw_frames, dark_frame, flat_field, seeing, anchors, taper):
    tile = lax.axis_index("tile")
    segment = lax.axis_index("segment")
    chip = tile // 2
    core = tile % 2
    n_sub = seeing.shape[1]
    width = raw_frames.shape[2]
    n_groups = width // GROUP
    frame = raw_frames[0]

    def along(step):
        return [(2 * z + k, 2 * (z + step) + k) for z in range(4) for k in range(2) if 0 <= z + step < 4]

    def right(x):
        return lax.ppermute(x, "tile", along(1))

    def left(x):
        return lax.ppermute(x, "tile", along(-1))

    def swap(x):
        return lax.ppermute(x, "tile", [(t, t ^ 1) for t in range(8)])

    own_rows = lax.dynamic_slice_in_dim(frame, 256 * chip, 512, 0)
    cut = [slice(GROUP * g, GROUP * g + GROUP) for g in range(n_groups)]

    gathered = []
    gate_r = gate_l = None
    for g in range(n_groups):
        send_r = frame[768:1280, cut[g]]
        send_l = frame[0:512, cut[g]]
        if gate_r is not None:
            send_r, gate_r = lax.optimization_barrier((send_r, gate_r))
            send_l, gate_l = lax.optimization_barrier((send_l, gate_l))
        r1 = right(send_r)
        l1 = left(send_l)
        gate_r, gate_l = r1, l1
        r2 = right(jnp.where(chip == 0, frame[256:768, cut[g]], r1))
        l2 = left(jnp.where(chip == 3, frame[512:1024, cut[g]], l1))
        middle = frame[512:768, cut[g]]
        r3 = right(jnp.where(chip == 1, jnp.concatenate([middle, r2[256:]], 0), r2))
        l3 = left(jnp.where(chip == 2, jnp.concatenate([middle, l2[:256]], 0), l2))
        own = own_rows[:, cut[g]]

        def pick(a, b, c, d):
            return jnp.where(chip == 0, a, jnp.where(chip == 1, b, jnp.where(chip == 2, c, d)))

        def cat(a, b):
            return jnp.concatenate([a, b], 0)

        stack = jnp.stack(
            [
                pick(own, r2, cat(r3[256:], r2[:256]), r3),
                pick(l1, own, cat(r3[:256], r1[:256]), r2),
                pick(l2, cat(l1[256:], l3[:256]), own, r1),
                pick(l3, cat(l2[256:], l3[256:]), l2, own),
            ]
        )
        upper = stack[:, :REGION]
        lower = stack[:, 128 : 128 + REGION]
        keep = jnp.where(core == 0, upper, lower)
        give = jnp.where(core == 0, lower, upper)
        gathered.append((keep, swap(give)))

    first_row = 128 * tile
    dark = lax.dynamic_slice_in_dim(dark_frame, first_row, REGION, 0).astype(jnp.float32)
    rate = 1.0 / lax.dynamic_slice_in_dim(flat_field, first_row, REGION, 0).astype(jnp.float32)
    mine = lax.dynamic_slice_in_dim(anchors, n_sub * tile, n_sub, 0)
    widths = lax.dynamic_slice_in_dim(taper, n_sub * tile, n_sub, 0)
    top = mine[:, 0] - first_row
    side = mine[:, 1] - 128 * jnp.arange(n_sub, dtype=jnp.int32)
    ramp = shifted_ramps(widths, jnp.zeros_like(side), S)[:, :, None] * shifted_ramps(
        widths, side, REGION
    )[:, None, :]
    cosine, sine = dft_tables(S)
    wave = jnp.concatenate([cosine, -sine], axis=1).astype(jnp.float32)
    wave = jnp.roll(jnp.concatenate([wave, wave], axis=0), 128, axis=0)
    wave = wave.reshape(2 * S, 4, 128).transpose(1, 0, 2)
    table = jnp.concatenate([cosine[:HALF], sine[:HALF]], axis=0)
    inverse = 1.0 / jnp.sum(seeing, axis=0)
    inverse = jnp.broadcast_to(inverse[:, None, None], (n_sub, 1, S))
    row = jnp.arange(S, dtype=jnp.int32)
    mirrored = segment >= 2
    turn = jnp.stack([(S - row) % S, S - 1 - row])
    turn = jnp.where(mirrored, turn, row[None, :])
    flip = (turn[:, None, :] == row[None, :, None]).astype(jnp.bfloat16)
    order = jnp.where(mirrored, 63 - row[:64], row[:64])
    mix = (row[None, :] % 64 == order[:, None]).astype(jnp.bfloat16)

    result = None
    for p in range(n_groups - 1):
        scal = jnp.concatenate(
            [
                jnp.stack([segment, 8 * segment, core, jnp.int32(2 * p)]),
                jnp.stack([top[2 * p], side[2 * p], top[2 * p + 1], side[2 * p + 1]]),
            ]
        ).astype(jnp.int32)
        own = (gathered[p][0], gathered[p + 1][0])
        far = (gathered[p][1], gathered[p + 1][1])
        partial = spectra(p, scal, seeing, own, far, dark, rate, ramp, wave, table)
        parts = [partial[:1]]
        for m in range(1, 4):
            parts.append(lax.ppermute(partial[m : m + 1], "segment", [(s, s ^ m) for s in range(4)]))
        result = finish(p, parts, flip, mix, inverse, result, n_sub)
    return tuple(result)


def solution(mesh):
    placed = (P(("segment", "tile"), None, None), P(), P(), P(None, "tile"), P(), P())
    by_rows = mesh.shape["tile"] == 8 and mesh.shape["segment"] == 4
    return jax.shard_map(
        local_rows if by_rows else local_any,
        mesh=mesh,
        in_specs=placed,
        out_specs=(P("tile", "segment", None), P("tile", None, "segment", None)),
        check_vma=False,
    )
```

```python
import functools
import math

import jax
import jax.numpy as jnp
from jax import lax
from jax.experimental import pallas as pl
from jax.experimental.pallas import tpu as pltpu
from jax.sharding import PartitionSpec as P

S = 256
COLUMN_BLOCKS = (4, 3, 2, 1)
REGION = 384
HALF = 136
VMEM_LIMIT = 60000 * 1024


def ramp_rows(taper, size):
    place = jnp.arange(size, dtype=jnp.float32)[None, :]
    width = taper.astype(jnp.float32)[:, None]
    left = jnp.where(place < width, 0.5 - 0.5 * jnp.cos(jnp.pi * (place + 0.5) / width), 1.0)
    return left * left[:, ::-1]


def dft_tables(size):
    steps = jnp.arange(size, dtype=jnp.int32)
    phase = steps[:, None] * steps[None, :] % size
    angle = 2.0 * jnp.pi * phase.astype(jnp.float32) / size
    factor = 1.0 / jnp.sqrt(jnp.float32(size))
    return (
        (jnp.cos(angle) * factor).astype(jnp.bfloat16),
        (jnp.sin(angle) * factor).astype(jnp.bfloat16),
    )


def first_pass(sub, cosine, sine):
    table = jnp.concatenate([cosine, -sine], axis=1)
    return jnp.einsum("fsxy,yk->fsxk", sub, table, preferred_element_type=jnp.float32).astype(
        jnp.bfloat16
    )


def second_pass(half, cosine, sine):
    size = cosine.shape[0]
    with_cos = jnp.einsum("ux,fsxk->fsuk", cosine, half, preferred_element_type=jnp.float32)
    with_sin = jnp.einsum("ux,fsxk->fsuk", sine, half, preferred_element_type=jnp.float32)
    real_part = with_cos[..., :size] + with_sin[..., size:]
    imag_part = with_cos[..., size:] - with_sin[..., :size]
    return (real_part, imag_part)


def local_any(raw_frames, dark_frame, flat_field, seeing, anchors, taper):
    size = S
    cosine, sine = dft_tables(size)
    ramps = ramp_rows(taper, size)
    calibrated = (
        raw_frames.astype(jnp.float32) - dark_frame.astype(jnp.float32)[None]
    ) / flat_field.astype(jnp.float32)[None]

    def cutout(anchor, ramp):
        start = jnp.zeros((), jnp.int32)
        cal = lax.dynamic_slice(
            calibrated, (start, anchor[0], anchor[1]), (calibrated.shape[0], size, size)
        )
        centered = cal - jnp.mean(cal, axis=(1, 2), keepdims=True)
        return (centered * (ramp[:, None] * ramp[None, :])[None]).astype(jnp.bfloat16)

    sub = jax.vmap(cutout, in_axes=(0, 0), out_axes=1)(anchors, ramps)
    received = lax.all_to_all(sub, "tile", split_axis=1, concat_axis=0, tiled=True)
    n_frames = received.shape[0]
    sub_dev = received.shape[1]
    block = math.gcd(n_frames, 8)
    n_blocks = n_frames // block
    segment_index = lax.axis_index("segment")
    weights = lax.dynamic_slice_in_dim(seeing, segment_index * n_frames, n_frames, 0)
    weight_sum = jnp.sum(seeing, axis=0)
    blocks = received.reshape((n_blocks, block) + received.shape[1:])
    weight_blocks = weights.reshape(n_blocks, block, sub_dev)

    def accumulate(carry, inputs):
        data, wblock = inputs
        half = first_pass(data, cosine, sine)
        real_part, imag_part = second_pass(half, cosine, sine)
        wgt = wblock[:, :, None, None]
        power_sum = carry[0] + jnp.sum(
            wgt * (real_part * real_part + imag_part * imag_part), axis=0
        )
        real_u = jnp.roll(real_part, -1, axis=2)
        imag_u = jnp.roll(imag_part, -1, axis=2)
        real_v = jnp.roll(real_part, -1, axis=3)
        imag_v = jnp.roll(imag_part, -1, axis=3)
        cross_sum = carry[1] + jnp.stack(
            [
                jnp.sum(wgt * (real_part * real_u + imag_part * imag_u), axis=0),
                jnp.sum(wgt * (imag_part * real_u - real_part * imag_u), axis=0),
                jnp.sum(wgt * (real_part * real_v + imag_part * imag_v), axis=0),
                jnp.sum(wgt * (imag_part * real_v - real_part * imag_v), axis=0),
            ],
            axis=1,
        )
        return ((power_sum, cross_sum), None)

    start_power = jnp.zeros((sub_dev, size, size), jnp.float32)
    start_cross = jnp.zeros((sub_dev, 4, size, size), jnp.float32)
    (power_sum, cross_sum), unused = lax.scan(
        accumulate, (start_power, start_cross), (blocks, weight_blocks)
    )
    power_rows, cross_rows = (
        lax.psum_scatter(
            power_sum.astype(jnp.bfloat16), "segment", scatter_dimension=1, tiled=True
        ).astype(jnp.float32),
        lax.psum_scatter(
            cross_sum.astype(jnp.bfloat16), "segment", scatter_dimension=2, tiled=True
        ).astype(jnp.float32),
    )
    power = power_rows / weight_sum[:, None, None]
    cross = cross_rows / weight_sum[:, None, None, None]
    return (power, cross)


def shifted_ramps(taper, offset, length):
    place = jnp.arange(length, dtype=jnp.int32)[None, :] - offset[:, None]
    inside = (place >= 0) & (place < S)
    width = taper.astype(jnp.float32)[:, None]

    def side(spot):
        spot = spot.astype(jnp.float32)
        rise = 0.5 - 0.5 * jnp.cos(jnp.pi * (spot + 0.5) / width)
        return jnp.where(spot < width, rise, 1.0)

    return jnp.where(inside, side(place) * side(S - 1 - place), 0.0)


def spectra_kernel(n_sub, first_sub, frames, tops, sides, spot, wgt, *refs):
    slabs = n_sub + 2
    raw = (refs[:slabs], refs[slabs : 2 * slabs])
    darks = refs[2 * slabs : 3 * slabs]
    rates = refs[3 * slabs : 4 * slabs]
    ramp, wave, table = refs[4 * slabs : 4 * slabs + 3]
    outs = refs[4 * slabs + 3 : 4 * slabs + 7]
    cal, shifted, real, imag, sums = refs[4 * slabs + 7 :]
    step = pl.program_id(0)
    segment = spot[0]

    @pl.when(step == 0)
    def _():
        sums[...] = jnp.zeros_like(sums)
        for j in range(n_sub):
            first = 128 - sides[first_sub + j]
            for m in range(4):
                shifted[j, :, 128 * m : 128 * m + 128] = wave[m, pl.ds(first, REGION), :].astype(
                    jnp.bfloat16
                )

    lane = lax.broadcasted_iota(jnp.int32, (1, 128), 1)
    last_lane = lax.broadcasted_iota(jnp.int32, (8, 128), 1) == 127
    for near in range(2):
        for c in range(slabs):
            cal[near, c] = (raw[near][c][0].astype(jnp.float32) - darks[c][...]) * rates[c][...]
    for near in range(2):
        frame = frames[4 * near + step]
        for j in range(n_sub):
            top = tops[first_sub + j]
            left = sides[first_sub + j]
            weight = wgt[frame, first_sub + j]
            pieces = [cal[near, j + m, pl.ds(top, S), :] for m in range(3)]
            total = [jnp.sum(piece, axis=0, keepdims=True) for piece in pieces]
            total = (
                jnp.where(lane >= left, total[0], 0.0)
                + total[1]
                + jnp.where(lane < left, total[2], 0.0)
            )
            mean = jnp.sum(total, axis=1, keepdims=True) * (1.0 / (S * S))
            sub = jnp.concatenate(
                [
                    ((piece - mean) * ramp[j, :, 128 * m : 128 * m + 128]).astype(jnp.bfloat16)
                    for m, piece in enumerate(pieces)
                ],
                axis=1,
            )
            half = jnp.dot(sub, shifted[j], preferred_element_type=jnp.float32).astype(jnp.bfloat16)
            both = jnp.dot(table[...], half, preferred_element_type=jnp.float32)
            for m in range(2):
                lo = slice(128 * m, 128 * m + 128)
                hi = slice(S + 128 * m, S + 128 * m + 128)
                real[near, j, m] = both[:HALF, lo] + both[HALF:, hi]
                imag[near, j, m] = both[:HALF, hi] - both[HALF:, lo]
            for r in range(0, HALF, 8):
                rows = slice(r, r + 8)
                re = [real[near, j, m, rows, :] for m in range(2)]
                im = [imag[near, j, m, rows, :] for m in range(2)]
                re_s = [pltpu.roll(x, 127, 1) for x in re]
                im_s = [pltpu.roll(x, 127, 1) for x in im]
                for m in range(2):
                    wre = re[m] * weight
                    wim = im[m] * weight
                    sums[j, 0, m, rows, :] += wre * re[m] + wim * im[m]
                    if r < 128:
                        below = slice(r + 1, r + 9)
                        re_u = real[near, j, m, below, :]
                        im_u = imag[near, j, m, below, :]
                        sums[j, 1, m, rows, :] += wre * re_u + wim * im_u
                        sums[j, 2, m, rows, :] += wim * re_u - wre * im_u
                    re_v = jnp.where(last_lane, re_s[1 - m], re_s[m])
                    im_v = jnp.where(last_lane, im_s[1 - m], im_s[m])
                    sums[j, 3, m, rows, :] += wre * re_v + wim * im_v
                    sums[j, 4, m, rows, :] += wim * re_v - wre * im_v

    @pl.when(step == pl.num_programs(0) - 1)
    def _():
        for slot in range(4):
            target = jnp.bitwise_xor(segment, slot)
            middle = (target == 1) | (target == 2)
            shared = jnp.where(middle, 64, 0)
            kept = shared + jnp.where(target >= 2, 1, 0)
            for j in range(n_sub):
                for plane in range(5):
                    first = shared if plane in (1, 2) else kept
                    for m in range(2):
                        outs[slot][j, plane, :, 128 * m : 128 * m + 128] = sums[
                            j, plane, m, pl.ds(first, 64), :
                        ].astype(jnp.bfloat16)


def spectra(first_sub, n_sub, tables, seeing, own, far, dark, rate, ramp, wave, table):
    slabs = n_sub + 2
    arrays = [a for a, c in own] + [a for a, c in far]
    specs = [pl.BlockSpec((1, REGION, 128), lambda i, *s, c=c: (i, 0, c)) for a, c in own + far]
    for const in (dark, rate):
        arrays += [const] * slabs
        specs += [
            pl.BlockSpec((REGION, 128), lambda i, *s, c=first_sub + k: (0, c)) for k in range(slabs)
        ]
    arrays += [ramp[first_sub : first_sub + n_sub], wave, table]
    specs += [
        pl.BlockSpec((n_sub, S, REGION), lambda i, *s: (0, 0, 0)),
        pl.BlockSpec(wave.shape, lambda i, *s: (0, 0, 0)),
        pl.BlockSpec(table.shape, lambda i, *s: (0, 0)),
    ]
    part = (n_sub, 5, 64, S)
    pairs = 8 * n_sub
    return pl.pallas_call(
        functools.partial(spectra_kernel, n_sub, first_sub),
        name="spectra",
        grid_spec=pltpu.PrefetchScalarGridSpec(
            num_scalar_prefetch=4,
            grid=(4,),
            in_specs=[pl.BlockSpec(memory_space=pltpu.SMEM)] + specs,
            out_specs=[pl.BlockSpec(part, lambda i, *s: (0, 0, 0, 0))] * 4,
            scratch_shapes=[
                pltpu.VMEM((2, slabs, REGION, 128), jnp.float32),
                pltpu.VMEM((n_sub, REGION, 2 * S), jnp.bfloat16),
                pltpu.VMEM((2, n_sub, 2, HALF, 128), jnp.float32),
                pltpu.VMEM((2, n_sub, 2, HALF, 128), jnp.float32),
                pltpu.VMEM((n_sub, 5, 2, HALF, 128), jnp.float32),
            ],
        ),
        out_shape=[jax.ShapeDtypeStruct(part, jnp.bfloat16)] * 4,
        cost_estimate=pl.CostEstimate(
            flops=pairs * 400_000_000, transcendentals=0, bytes_accessed=pairs * 1_000_000
        ),
        compiler_params=pltpu.CompilerParams(
            dimension_semantics=("arbitrary",), vmem_limit_bytes=VMEM_LIMIT
        ),
    )(*tables, seeing, *arrays)


def finish_kernel(n_sub, mine, got1, got2, got3, flip, mix, inverse, *refs):
    power, cross = refs[-2:]
    for j in range(n_sub):
        for plane in range(5):
            parts = jnp.concatenate([x[j, plane] for x in (mine, got1, got2, got3)], axis=0)
            turned = jnp.dot(
                parts, flip[1 if plane >= 3 else 0], preferred_element_type=jnp.float32
            ).astype(jnp.bfloat16)
            total = jnp.dot(mix[...], turned, preferred_element_type=jnp.float32)
            total = total * inverse[j]
            if plane == 0:
                power[j] = total
            else:
                cross[j, plane - 1] = total


def finish(first_sub, n_sub, parts, flip, mix, inverse, before, total_sub):
    arrays = [*parts, flip, mix, inverse[first_sub : first_sub + n_sub]]
    specs = [pl.BlockSpec(memory_space=pltpu.VMEM)] * 7
    aliases = {}
    if before is not None:
        specs += [pl.BlockSpec(memory_space=pl.ANY)] * 2
        arrays += before
        aliases = {7: 0, 8: 1}
    return pl.pallas_call(
        functools.partial(finish_kernel, n_sub),
        name="finish",
        grid=(1,),
        in_specs=specs,
        out_specs=[
            pl.BlockSpec((pl.Element(n_sub), pl.Element(64), pl.Element(S)), lambda i: (first_sub, 0, 0)),
            pl.BlockSpec(
                (pl.Element(n_sub), pl.Element(4), pl.Element(64), pl.Element(S)),
                lambda i: (first_sub, 0, 0, 0),
            ),
        ],
        out_shape=[
            jax.ShapeDtypeStruct((total_sub, 64, S), jnp.float32),
            jax.ShapeDtypeStruct((total_sub, 4, 64, S), jnp.float32),
        ],
        input_output_aliases=aliases,
        compiler_params=pltpu.CompilerParams(vmem_limit_bytes=VMEM_LIMIT),
    )(*arrays)


def local_rows(raw_frames, dark_frame, flat_field, seeing, anchors, taper):
    tile = lax.axis_index("tile")
    segment = lax.axis_index("segment")
    chip = tile // 2
    core = tile % 2
    total_sub = seeing.shape[1]
    frame = raw_frames[0]

    def send(x, to):
        pairs = [(2 * z + k, to(z, k)) for z in range(4) for k in range(2)]
        return lax.ppermute(x, "tile", pairs)

    def beside(x):
        return send(x, lambda z, k: 2 * (z ^ 1) + k)

    def two_on(x):
        return send(x, lambda z, k: 2 * ((z + 2) % 4) + k)

    def opposite(x):
        return send(x, lambda z, k: 2 * (3 - z) + k)

    def inner(x):
        return send(x, lambda z, k: 2 * (3 - z) + k if z in (1, 2) else 2 * z + 1 - k)

    def swap(x):
        return send(x, lambda z, k: 2 * z + 1 - k)

    def rows(first, length):
        return lax.dynamic_slice_in_dim(frame, first, length, 0)

    low = chip < 2
    edge = (chip == 0) | (chip == 3)
    to_beside = rows(256 * jnp.bitwise_xor(chip, 1), 512)
    to_two_on = rows(jnp.where(chip == 0, 768, jnp.where(chip == 1, 1024, jnp.where(chip == 2, 0, 256))), 256)
    to_opposite = rows(jnp.where(chip == 0, 1024, jnp.where(chip == 1, 768, jnp.where(chip == 2, 256, 0))), 256)
    own_rows = rows(256 * chip, 512)

    starts = []
    start = 0
    for blocks in COLUMN_BLOCKS:
        cut = slice(128 * start, 128 * (start + blocks))
        starts.append((start, cut))
        start += blocks

    first_hop = [
        (beside(to_beside[:, cut]), two_on(to_two_on[:, cut]), opposite(to_opposite[:, cut]))
        for start, cut in starts
    ]

    first_row = 128 * tile
    dark = lax.dynamic_slice_in_dim(dark_frame, first_row, REGION, 0).astype(jnp.float32)
    rate = 1.0 / lax.dynamic_slice_in_dim(flat_field, first_row, REGION, 0).astype(jnp.float32)
    mine = lax.dynamic_slice_in_dim(anchors, total_sub * tile, total_sub, 0)
    widths = lax.dynamic_slice_in_dim(taper, total_sub * tile, total_sub, 0)
    top = mine[:, 0] - first_row
    side = mine[:, 1] - 128 * jnp.arange(total_sub, dtype=jnp.int32)
    ramp = shifted_ramps(widths, jnp.zeros_like(side), S)[:, :, None] * shifted_ramps(
        widths, side, REGION
    )[:, None, :]
    cosine, sine = dft_tables(S)
    wave = jnp.concatenate([cosine, -sine], axis=1).astype(jnp.float32)
    wave = jnp.roll(jnp.concatenate([wave, wave], axis=0), 128, axis=0)
    wave = wave.reshape(2 * S, 4, 128).transpose(1, 0, 2)
    table = jnp.concatenate([cosine[:HALF], sine[:HALF]], axis=0)
    inverse = 1.0 / jnp.sum(seeing, axis=0)
    inverse = jnp.broadcast_to(inverse[:, None, None], (total_sub, 1, S))
    row = jnp.arange(S, dtype=jnp.int32)
    mirrored = segment >= 2
    turn = jnp.stack([(S - row) % S, S - 1 - row])
    turn = jnp.where(mirrored, turn, row[None, :])
    flip = (turn[:, None, :] == row[None, :, None]).astype(jnp.bfloat16)
    order = jnp.where(mirrored, 63 - row[:64], row[:64])
    mix = (row[None, :] % 64 == order[:, None]).astype(jnp.bfloat16)
    eight = jnp.arange(8, dtype=jnp.int32)
    slot = eight % 4
    source = jnp.where(slot == 1, jnp.bitwise_xor(chip, 1), chip)
    source = jnp.where(slot == 2, (chip + 2) % 4, source)
    source = jnp.where(slot == 3, 3 - chip, source)
    frames = 8 * segment + 2 * source + jnp.where(eight < 4, core, 1 - core)
    tables = (frames, top, side, jnp.where(eight == 0, segment, 0))

    own_slabs = []
    far_slabs = []
    done = 0
    result = None
    gate = None
    for g, (start, cut) in enumerate(starts):
        near, two, far = first_hop[g]
        if gate is not None:
            near, two, far, gate = lax.optimization_barrier((near, two, far, gate))
        f1 = beside(jnp.concatenate([far, two], 0))
        passed = jnp.where(low, near[256:], near[:256])
        f2 = inner(jnp.concatenate([passed, frame[512:768, cut]], 0))
        f = jnp.where(edge, f1, f2)
        two = jnp.where(low, jnp.concatenate([two, f[:256]], 0), jnp.concatenate([f[:256], two], 0))
        far = jnp.where(low, jnp.concatenate([far, f[256:]], 0), jnp.concatenate([f[256:], far], 0))
        stack = jnp.stack([own_rows[:, cut], near, two, far])
        upper = stack[:, :REGION]
        lower = stack[:, 128 : 128 + REGION]
        keep = jnp.where(core == 0, upper, lower)
        got = swap(jnp.where(core == 0, lower, upper))
        for c in range(COLUMN_BLOCKS[g]):
            own_slabs.append((keep, c))
            far_slabs.append((got, c))
        n_sub = len(own_slabs) - 2 - done
        span = slice(done, done + n_sub + 2)
        parts = spectra(
            done, n_sub, tables, seeing, own_slabs[span], far_slabs[span], dark, rate, ramp, wave, table
        )
        gate = parts[0]
        parts = [parts[0]] + [
            lax.ppermute(parts[m], "segment", [(s, s ^ m) for s in range(4)]) for m in range(1, 4)
        ]
        result = finish(done, n_sub, parts, flip, mix, inverse, result, total_sub)
        done += n_sub
    return tuple(result)


def solution(mesh):
    placed = (P(("segment", "tile"), None, None), P(), P(), P(None, "tile"), P(), P())
    by_rows = mesh.shape["tile"] == 8 and mesh.shape["segment"] == 4
    return jax.shard_map(
        local_rows if by_rows else local_any,
        mesh=mesh,
        in_specs=placed,
        out_specs=(P("tile", "segment", None), P("tile", None, "segment", None)),
        check_vma=False,
    )
```
